32 devices in a mesh: layer: 4 (over x, core), dp: 8 (over z, y).
Axes of the slice: x: 2, y: 2, z: 4, core: 2. Of those that a mesh axis runs over, the one named last changes fastest.
Arguments:
- out_grads: bfloat16 [4, 128, 16384], P('layer', None, 'dp'), may hold values from -3 to 3
- in_acts: bfloat16 [4, 128, 4096], P('layer', None, 'dp'), may hold values from -3 to 3
- out_basis: bfloat16 [4, 16384, 16384], P('layer', None, 'dp'), may hold values from -0.046875 to 0.046875
- in_basis: bfloat16 [4, 4096, 4096], P('layer', None, 'dp'), may hold values from -0.09375 to 0.09375
- eigenvalues: bfloat16 [4, 16384, 4096], P('layer', 'dp'), may hold values from 0.5 to 50
- out_store: bfloat16 [4, 16, 32, 16384], P('layer', 'dp'), may hold values from -0.046875 to 0.046875
- in_store: bfloat16 [4, 16, 32, 4096], P('layer', 'dp'), may hold values from -0.09375 to 0.09375
- counts: int32 [16], P('dp'), may hold values from 1 to 4096
- winners: int32 [4, 6], replicated, may hold values from 0 to 15
Outputs:
- influence: float32 [4, 6, 32], replicated
The draws below stay inside these ranges and needn't reach their ends.
All inputs are finite; a program needn't handle non-finite values.
Results may differ from the reference program's by a relative error of at most 0.0055.
Values may be sent and summed in bfloat16 or wider, within the bound.
A program may use at most 192 MiB of HBM per device.

```python
import math
import jax
import jax.numpy as jnp
import numpy as np

D = 4096
F = 16384
NQ = 4
TQ = 32
WIN = 6
R = 32
SPAN = 128
LAYERS = 4
NSEQ = 16


def set_ends(drawn, stream_key, least, largest):
    spot = [jax.random.randint(jax.random.fold_in(stream_key, axis), (), 0, length) for axis, length in enumerate(drawn.shape)]
    widest = drawn.shape.index(max(drawn.shape))
    next_to = spot[:widest] + [(spot[widest] + 1) % drawn.shape[widest]] + spot[widest + 1:]
    return drawn.at[tuple(spot)].set(least).at[tuple(next_to)].set(largest)


def steps_of(own_key, extent, pieces, low, top_value):
    level, own = 1.0, jax.random.fold_in(own_key, 6)
    for axis_at, blocks in pieces:
        heights = jnp.exp(jax.random.uniform(jax.random.fold_in(own, axis_at), (blocks,), jnp.float32, low / len(pieces), top_value / len(pieces)))
        level = level * jnp.repeat(heights, extent[axis_at] // blocks).reshape([-1 if axis == axis_at else 1 for axis in range(len(extent))])
    return level


def cumulative_ranks(number_of, slope):
    portions = [(1 << 20) // math.isqrt(grade ** slope) + 1 for grade in range(1, number_of + 1)]
    spread = 1 + sum(portions) // (1 << 30)
    return np.cumsum(np.array([max(1, weight // spread) for weight in portions]))


def ranked(key, shape, number_of, lean):
    grid = cumulative_ranks(number_of, lean)
    pick = jax.random.randint(jax.random.fold_in(key, 1), shape, 0, int(grid[number_of - 1]))
    standing = jnp.searchsorted(jnp.asarray(grid, jnp.int32), pick, side="right")
    return jax.random.permutation(jax.random.fold_in(key, 2), number_of)[standing].astype(jnp.int32)


def normal_values(own_key, shape, width, limit, shards=(), kind=jnp.bfloat16):
    level = steps_of(own_key, shape, shards, -0.22, 0.18) if shards else 1.0
    values = jax.random.normal(own_key, shape, jnp.float32) * width * level
    return jnp.minimum(jnp.maximum(values, -limit), limit).astype(kind)


def setup_inputs(seed: int = 0) -> dict:
    keys = jax.random.split(jax.random.key(seed), 10)
    return {
        "out_grads": normal_values(keys[0], (LAYERS, NQ * TQ, F), 0.5, 3.0, ((0, 4), (2, 8))),
        "in_acts": normal_values(keys[1], (LAYERS, NQ * TQ, D), 0.5, 3.0, ((0, 4), (2, 8))),
        "out_basis": normal_values(keys[2], (LAYERS, F, F), F ** -0.5, 0.046875, ((0, 4), (2, 8))),
        "in_basis": normal_values(keys[3], (LAYERS, D, D), D ** -0.5, 0.09375, ((0, 4), (2, 8))),
        "eigenvalues": jnp.clip(jnp.exp(math.log(50.0) - 4.6051702 * jax.random.uniform(keys[4], (LAYERS, F, D), jnp.float32) ** steps_of(keys[4], (LAYERS, F, D), ((0, 4), (1, 8)), -0.2, 0.2)), 0.5, 50.0).astype(jnp.bfloat16),
        "out_store": normal_values(keys[5], (LAYERS, NSEQ, R, F), F ** -0.5, 0.046875, ((0, 4), (1, 8))),
        "in_store": normal_values(keys[6], (LAYERS, NSEQ, R, D), D ** -0.5, 0.09375, ((0, 4), (1, 8))),
        "counts": set_ends(jax.random.randint(keys[7], (NSEQ,), 1, R * SPAN + 1), jax.random.fold_in(keys[7], 1), 1, R * SPAN).astype(jnp.int32),
        "winners": set_ends(ranked(keys[8], (NQ, WIN), NSEQ, 2), jax.random.fold_in(keys[8], 3), 0, NSEQ - 1).astype(jnp.int32),
    }


damping = 0.1


def reference(out_grads, in_acts, out_basis, in_basis, eigenvalues, out_store, in_store, counts, winners):
    alive = (jnp.arange(R, dtype=jnp.int32)[None, :] * SPAN < counts[:, None]).astype(jnp.bfloat16)
    totals = jnp.zeros((NQ, WIN * R), jnp.float32)
    for layer_index in range(LAYERS):
        turned_out = jnp.dot(out_grads[layer_index], out_basis[layer_index], preferred_element_type=jnp.float32).astype(jnp.bfloat16)
        turned_in = jnp.dot(in_acts[layer_index], in_basis[layer_index], preferred_element_type=jnp.float32).astype(jnp.bfloat16)
        masked = in_store[layer_index] * alive[:, :, None]
        divisor = eigenvalues[layer_index].astype(jnp.float32) + damping
        for query_index in range(NQ):
            left = turned_out[query_index * TQ:(query_index + 1) * TQ]
            right = turned_in[query_index * TQ:(query_index + 1) * TQ]
            product = jnp.dot(left.T, right, preferred_element_type=jnp.float32)
            precond = (product / divisor).astype(jnp.bfloat16)
            chosen = winners[query_index]
            right_rows = masked[chosen].reshape(WIN * R, D)
            left_rows = out_store[layer_index][chosen].reshape(WIN * R, F)
            mapped = jnp.dot(precond, right_rows.T, preferred_element_type=jnp.float32)
            terms = jnp.sum(mapped.T * left_rows.astype(jnp.float32), axis=1)
            totals = totals.at[query_index].add(terms)
    return totals.reshape(NQ, WIN, R)
```

```python
import functools

import jax
import jax.numpy as jnp
from jax import lax
from jax.experimental import pallas as pl
from jax.experimental.pallas import tpu as pltpu
from jax.sharding import PartitionSpec as P

NQ = 4
TQ = 32
WIN = 6
R = 32
SPAN = 128
COLS = 256
BUFFERS = 3
MESH = pl.DeviceIdType.MESH


damping = 0.1


class Gather:
    def __init__(self, n, me, own, full, send_sem, recv_sem):
        self.n, self.nh = n, n // 2
        self.h, self.y = me // 2, lax.rem(me, 2)
        self.own, self.full, self.send_sem, self.recv_sem = own, full, send_sem, recv_sem
        self.half = full.shape[1] // 2
        small = (self.nh - 1) // 2
        large = self.nh - 1 - small
        self.reach = (((-1, small), (1, large)), ((-1, large), (1, small)))
        self.waves = large
        self.pending = []

    def index(self, dh, other):
        return lax.rem(self.h + dh + self.nh, self.nh) * 2 + (1 - self.y if other else self.y)

    def place(self, ref, part):
        return ref.at[pl.ds(part * self.half, self.half)]

    def send(self, part, dh, way):
        j = self.index(dh, False)
        if way == 0:
            to, slot = self.index(0, True), 2
        else:
            to, slot = self.index(way, False), (way + 1) // 2
        target = self.place(self.full.at[j], part)
        source = self.place(self.own, part) if dh == 0 else target
        copy = pltpu.make_async_remote_copy(
            src_ref=source,
            dst_ref=target,
            send_sem=self.send_sem.at[part, dh + self.nh, slot],
            recv_sem=self.recv_sem.at[part, j],
            device_id={"dp": to},
            device_id_type=MESH,
        )
        copy.start()
        self.pending.append(copy)

    def wait(self, part, dh, other):
        j = self.index(dh, other)
        target = self.place(self.full.at[j], part)
        pltpu.make_async_remote_copy(
            src_ref=target,
            dst_ref=target,
            send_sem=self.send_sem.at[part, 0, 0],
            recv_sem=self.recv_sem.at[part, j],
            device_id={"dp": self.index(0, True)},
            device_id_type=MESH,
        ).wait_recv()

    def start(self):
        for part in (0, 1):
            for way, reach in self.reach[part]:
                if reach > 0:
                    self.send(part, 0, way)
            self.send(part, 0, 0)

    def wave(self, w):
        for part in (0, 1):
            for way, reach in self.reach[part]:
                if w <= reach:
                    dh = -way * w
                    self.wait(part, dh, False)
                    if w < reach:
                        self.send(part, dh, way)
                    self.send(part, dh, 0)

    def finish(self):
        for part in (0, 1):
            self.wait(part, 0, True)
        for w in range(1, self.waves + 1):
            for part in (0, 1):
                for way, reach in self.reach[part]:
                    if w <= reach:
                        self.wait(part, -way * w, True)

    def drain(self):
        for copy in self.pending:
            copy.wait_send()


def rotate_kernel(
    n,
    og_ref,
    ia_ref,
    mk_ref,
    os_ref,
    ob_ref,
    ib_ref,
    to_ref,
    ti_ref,
    mk_all,
    os_all,
    og_all,
    ia_all,
    ti_own,
    ib_buf,
    ob_buf,
    acc,
    local_sem,
    ob_sem,
    og_send,
    og_recv,
    ia_send,
    ia_recv,
    mk_send,
    mk_recv,
    ti_send,
    ti_recv,
    os_send,
    os_recv,
):
    me = lax.axis_index("dp")
    nh = n // 2
    h, y = me // 2, lax.rem(me, 2)
    depth = og_ref.shape[1]
    width = ob_ref.shape[1]
    in_depth = ia_ref.shape[1]

    def chunk_index(k):
        return lax.rem(h + lax.rem(k, nh), nh) * 2 + lax.rem(y + k // nh, 2)

    def fetch(k, slot):
        rows = pl.ds(pl.multiple_of(chunk_index(k) * depth, depth), depth)
        return pltpu.make_async_copy(ob_ref.at[rows], ob_buf.at[slot], ob_sem.at[slot])

    locals_ = [
        pltpu.make_async_copy(ia_ref, ia_all.at[me], local_sem.at[0]),
        pltpu.make_async_copy(og_ref, og_all.at[me], local_sem.at[1]),
        pltpu.make_async_copy(ib_ref, ib_buf, local_sem.at[2]),
        pltpu.make_async_copy(mk_ref, mk_all.at[me], local_sem.at[3]),
        pltpu.make_async_copy(
            os_ref.at[:, pl.ds(pl.multiple_of(me * width, width), width)],
            os_all.at[me],
            local_sem.at[4],
        ),
    ]
    for copy in locals_:
        copy.start()
    for k in range(min(BUFFERS, n)):
        fetch(k, k).start()

    barrier = pltpu.get_barrier_semaphore()

    @pl.loop(1, n)
    def _(d):
        pl.semaphore_signal(
            barrier, inc=1, device_id={"dp": lax.rem(me + d, n)}, device_id_type=MESH
        )

    pl.semaphore_wait(barrier, n - 1)

    ia = Gather(n, me, ia_ref, ia_all, ia_send, ia_recv)
    og = Gather(n, me, og_ref, og_all, og_send, og_recv)
    mk = Gather(n, me, mk_ref, mk_all, mk_send, mk_recv)
    ti = Gather(n, me, ti_own, ti_ref, ti_send, ti_recv)

    def slices(d):
        to = lax.rem(me + d, n)
        return pltpu.make_async_remote_copy(
            src_ref=os_ref.at[:, pl.ds(pl.multiple_of(to * width, width), width)],
            dst_ref=os_all.at[me],
            send_sem=os_send.at[d],
            recv_sem=os_recv.at[me],
            device_id={"dp": to},
            device_id_type=MESH,
        )

    def dots(low, high):
        def one(k, carry):
            slot = lax.rem(k, BUFFERS)
            fetch(k, slot).wait()
            j = chunk_index(k)

            @pl.loop(0, width // COLS)
            def _(c):
                cols = pl.ds(pl.multiple_of(c * COLS, COLS), COLS)
                acc[:, cols] += jnp.dot(
                    og_all[j], ob_buf[slot, :, cols], preferred_element_type=jnp.float32
                )

            @pl.when(k + BUFFERS < n)
            def _():
                fetch(k + BUFFERS, slot).start()

            return carry

        lax.fori_loop(low, high, one, 0)

    ia.start()
    og.start()
    acc[...] = jnp.zeros_like(acc)
    for copy in locals_:
        copy.wait()
    for w in range(1, ia.waves + 1):
        ia.wave(w)
    ia.finish()
    og.wave(1)
    mk.start()

    def rotate(j, total):
        rows = pl.ds(pl.multiple_of(j * in_depth, in_depth), in_depth)
        return total + jnp.dot(ia_all[j], ib_buf[rows, :], preferred_element_type=jnp.float32)

    total = lax.fori_loop(0, n, rotate, jnp.zeros((ia_ref.shape[0], ib_ref.shape[1]), jnp.float32))
    ti_own[...] = total.astype(ti_own.dtype)
    own_turned = pltpu.make_async_copy(ti_own, ti_ref.at[me], local_sem.at[5])
    own_turned.start()
    ti.start()
    for w in range(2, og.waves + 1):
        og.wave(w)
    dots(0, 1)
    og.finish()
    mk.wave(1)
    ti.wave(1)
    dots(1, nh)
    for w in range(2, mk.waves + 1):
        mk.wave(w)
        ti.wave(w)

    @pl.loop(1, n)
    def _(d):
        slices(d).start()

    dots(nh, n)
    to_ref[...] = acc[...].astype(to_ref.dtype)
    mk.finish()
    ti.finish()
    own_turned.wait()
    for gather in (ia, og, mk, ti):
        gather.drain()

    @pl.loop(1, n)
    def _(d):
        slices(d).wait_send()
        source = lax.rem(me + d, n)
        pltpu.make_async_remote_copy(
            src_ref=os_all.at[source],
            dst_ref=os_all.at[source],
            send_sem=os_send.at[0],
            recv_sem=os_recv.at[source],
            device_id={"dp": source},
            device_id_type=MESH,
        ).wait_recv()


def rotate(n, og, ia, mk, out_store, out_basis, in_basis):
    tokens, depth = og.shape
    in_depth = ia.shape[1]
    width, in_width = out_basis.shape[1], in_basis.shape[1]
    rows, full = mk.shape
    nh = n // 2
    sends = pltpu.SemaphoreType.DMA((2, 2 * nh, 3))
    recvs = pltpu.SemaphoreType.DMA((2, n))
    dtype = og.dtype
    anywhere = pl.BlockSpec(memory_space=pl.ANY)
    vmem = pl.BlockSpec(memory_space=pltpu.VMEM)
    return pl.pallas_call(
        functools.partial(rotate_kernel, n),
        out_shape=(
            jax.ShapeDtypeStruct((tokens, width), dtype),
            jax.ShapeDtypeStruct((n, tokens, in_width), dtype),
            jax.ShapeDtypeStruct((n, rows, full), dtype),
            jax.ShapeDtypeStruct((n, rows, width), dtype),
        ),
        in_specs=[anywhere] * 6,
        out_specs=(vmem,) * 4,
        scratch_shapes=[
            pltpu.VMEM((n, tokens, depth), dtype),
            pltpu.VMEM((n, tokens, in_depth), dtype),
            pltpu.VMEM((tokens, in_width), dtype),
            pltpu.VMEM(in_basis.shape, dtype),
            pltpu.VMEM((BUFFERS, depth, width), dtype),
            pltpu.VMEM((tokens, width), jnp.float32),
            pltpu.SemaphoreType.DMA((6,)),
            pltpu.SemaphoreType.DMA((BUFFERS,)),
            sends,
            recvs,
            sends,
            recvs,
            sends,
            recvs,
            sends,
            recvs,
            pltpu.SemaphoreType.DMA((n,)),
            pltpu.SemaphoreType.DMA((n,)),
        ],
        compiler_params=pltpu.CompilerParams(
            collective_id=0, has_side_effects=True, vmem_limit_bytes=60 << 20
        ),
    )(og, ia, mk, out_store, out_basis, in_basis)


def total_kernel(n, layers, x_ref, out_ref, dp_slots, sub_total, layer_slots, local_sem, dp_send, dp_recv, layer_send, layer_recv):
    me, my_layer = lax.axis_index("dp"), lax.axis_index("layer")
    barrier = pltpu.get_barrier_semaphore()
    for axis, size, at in (("dp", n, me), ("layer", layers, my_layer)):

        @pl.loop(1, size)
        def _(d):
            pl.semaphore_signal(
                barrier, inc=1, device_id={axis: lax.rem(at + d, size)}, device_id_type=MESH
            )

    pl.semaphore_wait(barrier, n + layers - 2)

    def stage(axis, size, at, source, slots, send_sem, recv_sem):
        own = pltpu.make_async_copy(source, slots.at[at], local_sem)
        own.start()

        def push(d, slot):
            return pltpu.make_async_remote_copy(
                src_ref=source,
                dst_ref=slots.at[slot],
                send_sem=send_sem.at[d],
                recv_sem=recv_sem.at[slot],
                device_id={axis: lax.rem(at + d, size)},
                device_id_type=MESH,
            )

        @pl.loop(1, size)
        def _(d):
            push(d, at).start()

        own.wait()

        @pl.loop(1, size)
        def _(d):
            push(d, lax.rem(at + d, size)).wait()

        return lax.fori_loop(
            0, size, lambda i, total: total + slots[i], jnp.zeros(slots.shape[1:], slots.dtype)
        )

    sub_total[...] = stage("dp", n, me, x_ref, dp_slots, dp_send, dp_recv)
    out_ref[...] = stage("layer", layers, my_layer, sub_total, layer_slots, layer_send, layer_recv)


def total(n, layers, x):
    vmem = pl.BlockSpec(memory_space=pltpu.VMEM)
    return pl.pallas_call(
        functools.partial(total_kernel, n, layers),
        out_shape=jax.ShapeDtypeStruct(x.shape, x.dtype),
        in_specs=[vmem],
        out_specs=vmem,
        scratch_shapes=[
            pltpu.VMEM((n, *x.shape), x.dtype),
            pltpu.VMEM(x.shape, x.dtype),
            pltpu.VMEM((layers, *x.shape), x.dtype),
            pltpu.SemaphoreType.DMA,
            pltpu.SemaphoreType.DMA((n,)),
            pltpu.SemaphoreType.DMA((n,)),
            pltpu.SemaphoreType.DMA((layers,)),
            pltpu.SemaphoreType.DMA((layers,)),
        ],
        compiler_params=pltpu.CompilerParams(
            collective_id=1, has_side_effects=True, vmem_limit_bytes=8 << 20
        ),
    )(x)


def on_device(
    n, layers,
    out_grads, in_acts, out_basis, in_basis, eigenvalues, out_store, in_store, counts, winners
):
    _, seqs, tokens, features = in_store.shape
    width = out_basis.shape[2]
    alive = (jnp.arange(R, dtype=jnp.int32)[None, :] * SPAN < counts[:, None]).astype(jnp.bfloat16)
    masked = in_store[0] * alive[:, :, None]
    turned_out, turned_in, in_whole, out_slices = rotate(
        n,
        out_grads[0],
        in_acts[0],
        masked.reshape(seqs * tokens, features),
        out_store[0].reshape(seqs * tokens, out_store.shape[3]),
        out_basis[0],
        in_basis[0],
    )
    in_whole = in_whole.reshape(n * seqs, tokens, features)
    out_slices = out_slices.reshape(n * seqs, tokens, width)
    left = turned_out.reshape(NQ, TQ, width)
    right = turned_in.reshape(n, NQ, TQ, in_basis.shape[2]).transpose(1, 2, 0, 3).reshape(NQ, TQ, features)
    product = jnp.einsum("qtf,qtd->qfd", left, right, preferred_element_type=jnp.float32)
    divisor = eigenvalues[0].astype(jnp.float32) + damping
    precond = (product / divisor[None]).astype(jnp.bfloat16)
    chosen = winners.reshape(NQ * WIN)
    left_rows = jnp.take(out_slices, chosen, axis=0).reshape(NQ, WIN * R, width)
    right_rows = jnp.take(in_whole, chosen, axis=0).reshape(NQ, WIN * R, features)
    mapped = jnp.einsum("qfd,qkd->qkf", precond, right_rows, preferred_element_type=jnp.float32)
    partial_value = jnp.sum(mapped * left_rows.astype(jnp.float32), axis=2)
    return total(n, layers, partial_value).reshape(NQ, WIN, R)


def solution(mesh):
    placed = (
        P("layer", None, "dp"),
        P("layer", None, "dp"),
        P("layer", None, "dp"),
        P("layer", None, "dp"),
        P("layer", "dp", None),
        P("layer", "dp", None, None),
        P("layer", "dp", None, None),
        P("dp"),
        P(),
    )
    body = functools.partial(on_device, mesh.shape["dp"], mesh.shape["layer"])
    return jax.shard_map(body, mesh=mesh, in_specs=placed, out_specs=P(), check_vma=False)
```

```python
import functools

import jax
import jax.numpy as jnp
from jax import lax
from jax.experimental import pallas as pl
from jax.experimental.pallas import tpu as pltpu
from jax.sharding import PartitionSpec as P

NQ = 4
TQ = 32
WIN = 6
R = 32
SPAN = 128
COLS = 256
TILE = 256
SPAN_COLS = 1024
BUFFERS = 3
MESH = pl.DeviceIdType.MESH


damping = 0.1


class Gather:
    def __init__(self, n, me, own, full, send_sem, recv_sem):
        self.n, self.nh = n, n // 2
        self.h, self.y = me // 2, lax.rem(me, 2)
        self.own, self.full, self.send_sem, self.recv_sem = own, full, send_sem, recv_sem
        self.half = full.shape[1] // 2
        small = (self.nh - 1) // 2
        large = self.nh - 1 - small
        self.reach = (((-1, small), (1, large)), ((-1, large), (1, small)))
        self.waves = large
        self.pending = []

    def index(self, dh, other):
        return lax.rem(self.h + dh + self.nh, self.nh) * 2 + (1 - self.y if other else self.y)

    def place(self, ref, part):
        return ref.at[pl.ds(part * self.half, self.half)]

    def send(self, part, dh, way):
        j = self.index(dh, False)
        if way == 0:
            to, slot = self.index(0, True), 2
        else:
            to, slot = self.index(way, False), (way + 1) // 2
        target = self.place(self.full.at[j], part)
        source = self.place(self.own, part) if dh == 0 else target
        copy = pltpu.make_async_remote_copy(
            src_ref=source,
            dst_ref=target,
            send_sem=self.send_sem.at[part, dh + self.nh, slot],
            recv_sem=self.recv_sem.at[part, j],
            device_id={"dp": to},
            device_id_type=MESH,
        )
        copy.start()
        self.pending.append(copy)

    def wait(self, part, dh, other):
        j = self.index(dh, other)
        target = self.place(self.full.at[j], part)
        pltpu.make_async_remote_copy(
            src_ref=target,
            dst_ref=target,
            send_sem=self.send_sem.at[part, 0, 0],
            recv_sem=self.recv_sem.at[part, j],
            device_id={"dp": self.index(0, True)},
            device_id_type=MESH,
        ).wait_recv()

    def start(self):
        for part in (0, 1):
            for way, reach in self.reach[part]:
                if reach > 0:
                    self.send(part, 0, way)
            self.send(part, 0, 0)

    def wave(self, w):
        for part in (0, 1):
            for way, reach in self.reach[part]:
                if w <= reach:
                    dh = -way * w
                    self.wait(part, dh, False)
                    if w < reach:
                        self.send(part, dh, way)
                    self.send(part, dh, 0)

    def finish(self):
        for part in (0, 1):
            self.wait(part, 0, True)
        for w in range(1, self.waves + 1):
            for part in (0, 1):
                for way, reach in self.reach[part]:
                    if w <= reach:
                        self.wait(part, -way * w, True)

    def drain(self):
        for copy in self.pending:
            copy.wait_send()


def rotate_kernel(
    n,
    og_ref,
    ia_ref,
    mk_ref,
    ob_ref,
    ib_ref,
    to_ref,
    ti_ref,
    mk_all,
    og_all,
    ia_all,
    ti_own,
    ib_buf,
    ob_buf,
    acc,
    local_sem,
    ob_sem,
    og_send,
    og_recv,
    ia_send,
    ia_recv,
    mk_send,
    mk_recv,
    ti_send,
    ti_recv,
):
    me = lax.axis_index("dp")
    nh = n // 2
    h, y = me // 2, lax.rem(me, 2)
    depth = og_ref.shape[1]
    width = ob_ref.shape[1]
    in_depth = ia_ref.shape[1]

    def chunk_index(k):
        return lax.rem(h + lax.rem(k, nh), nh) * 2 + lax.rem(y + k // nh, 2)

    def fetch(k, slot):
        rows = pl.ds(pl.multiple_of(chunk_index(k) * depth, depth), depth)
        return pltpu.make_async_copy(ob_ref.at[rows], ob_buf.at[slot], ob_sem.at[slot])

    locals_ = [
        pltpu.make_async_copy(ia_ref, ia_all.at[me], local_sem.at[0]),
        pltpu.make_async_copy(og_ref, og_all.at[me], local_sem.at[1]),
        pltpu.make_async_copy(ib_ref, ib_buf, local_sem.at[2]),
        pltpu.make_async_copy(mk_ref, mk_all.at[me], local_sem.at[3]),
    ]
    for copy in locals_:
        copy.start()
    for k in range(min(BUFFERS, n)):
        fetch(k, k).start()

    barrier = pltpu.get_barrier_semaphore()

    @pl.loop(1, n)
    def _(d):
        pl.semaphore_signal(
            barrier, inc=1, device_id={"dp": lax.rem(me + d, n)}, device_id_type=MESH
        )

    pl.semaphore_wait(barrier, n - 1)

    ia = Gather(n, me, ia_ref, ia_all, ia_send, ia_recv)
    og = Gather(n, me, og_ref, og_all, og_send, og_recv)
    mk = Gather(n, me, mk_ref, mk_all, mk_send, mk_recv)
    ti = Gather(n, me, ti_own, ti_ref, ti_send, ti_recv)

    def dots(low, high):
        def one(k, carry):
            slot = lax.rem(k, BUFFERS)
            fetch(k, slot).wait()
            j = chunk_index(k)

            @pl.loop(0, width // COLS)
            def _(c):
                cols = pl.ds(pl.multiple_of(c * COLS, COLS), COLS)
                acc[:, cols] += jnp.dot(
                    og_all[j], ob_buf[slot, :, cols], preferred_element_type=jnp.float32
                )

            @pl.when(k + BUFFERS < n)
            def _():
                fetch(k + BUFFERS, slot).start()

            return carry

        lax.fori_loop(low, high, one, 0)

    ia.start()
    og.start()
    acc[...] = jnp.zeros_like(acc)
    for copy in locals_:
        copy.wait()
    for w in range(1, ia.waves + 1):
        ia.wave(w)
    ia.finish()
    og.wave(1)
    mk.start()

    def rotate(j, total):
        rows = pl.ds(pl.multiple_of(j * in_depth, in_depth), in_depth)
        return total + jnp.dot(ia_all[j], ib_buf[rows, :], preferred_element_type=jnp.float32)

    total = lax.fori_loop(0, n, rotate, jnp.zeros((ia_ref.shape[0], ib_ref.shape[1]), jnp.float32))
    ti_own[...] = total.astype(ti_own.dtype)
    own_turned = pltpu.make_async_copy(ti_own, ti_ref.at[me], local_sem.at[5])
    own_turned.start()
    ti.start()
    for w in range(2, og.waves + 1):
        og.wave(w)
    dots(0, 1)
    og.finish()
    mk.wave(1)
    ti.wave(1)
    dots(1, nh)
    for w in range(2, mk.waves + 1):
        mk.wave(w)
        ti.wave(w)

    dots(nh, n)
    to_ref[...] = acc[...].astype(to_ref.dtype)
    mk.finish()
    ti.finish()
    own_turned.wait()
    for gather in (ia, og, mk, ti):
        gather.drain()


def rotate(n, og, ia, mk, out_basis, in_basis):
    tokens, depth = og.shape
    in_depth = ia.shape[1]
    width, in_width = out_basis.shape[1], in_basis.shape[1]
    rows, full = mk.shape
    nh = n // 2
    sends = pltpu.SemaphoreType.DMA((2, 2 * nh, 3))
    recvs = pltpu.SemaphoreType.DMA((2, n))
    dtype = og.dtype
    anywhere = pl.BlockSpec(memory_space=pl.ANY)
    vmem = pl.BlockSpec(memory_space=pltpu.VMEM)
    return pl.pallas_call(
        functools.partial(rotate_kernel, n),
        out_shape=(
            jax.ShapeDtypeStruct((tokens, width), dtype),
            jax.ShapeDtypeStruct((n, tokens, in_width), dtype),
            jax.ShapeDtypeStruct((n, rows, full), dtype),
        ),
        in_specs=[anywhere] * 5,
        out_specs=(vmem,) * 3,
        scratch_shapes=[
            pltpu.VMEM((n, tokens, depth), dtype),
            pltpu.VMEM((n, tokens, in_depth), dtype),
            pltpu.VMEM((tokens, in_width), dtype),
            pltpu.VMEM(in_basis.shape, dtype),
            pltpu.VMEM((BUFFERS, depth, width), dtype),
            pltpu.VMEM((tokens, width), jnp.float32),
            pltpu.SemaphoreType.DMA((6,)),
            pltpu.SemaphoreType.DMA((BUFFERS,)),
            sends,
            recvs,
            sends,
            recvs,
            sends,
            recvs,
            sends,
            recvs,
        ],
        compiler_params=pltpu.CompilerParams(
            collective_id=0, has_side_effects=True, vmem_limit_bytes=60 << 20
        ),
    )(og, ia, mk, out_basis, in_basis)


def score_kernel(
    n,
    layers,
    winners_ref,
    to_ref,
    ti_ref,
    mk_ref,
    eig_ref,
    os_ref,
    out_ref,
    os_all,
    ti_full,
    rows,
    eig_buf,
    turned,
    mapped,
    lanes,
    partial,
    dp_slots,
    sub_total,
    layer_slots,
    eig_sem,
    local_sem,
    os_send,
    os_recv,
    dp_send,
    dp_recv,
    layer_send,
    layer_recv,
):
    me, my_layer = lax.axis_index("dp"), lax.axis_index("layer")
    width = to_ref.shape[1]
    tiles = width // TILE
    features = eig_ref.shape[1]
    in_width = ti_ref.shape[2]
    seqs = os_ref.shape[0]
    winning = rows.shape[0]
    span = min(SPAN_COLS, features)

    def fetch(t, slot):
        at = pl.ds(pl.multiple_of(t * TILE, TILE), TILE)
        return pltpu.make_async_copy(eig_ref.at[at], eig_buf.at[slot], eig_sem.at[slot])

    for t in range(min(2, tiles)):
        fetch(t, t).start()

    def block(j):
        return pl.ds(pl.multiple_of(j * width, width), width)

    own_slice = pltpu.make_async_copy(
        os_ref.at[:, :, block(me)], os_all.at[pl.ds(me * seqs, seqs)], local_sem.at[0]
    )
    own_slice.start()

    barrier = pltpu.get_barrier_semaphore()
    for axis, size, at in (("dp", n, me), ("layer", layers, my_layer)):

        @pl.loop(1, size)
        def _(d):
            pl.semaphore_signal(
                barrier, inc=1, device_id={axis: lax.rem(at + d, size)}, device_id_type=MESH
            )

    pl.semaphore_wait(barrier, n + layers - 2)

    def slices(d, source):
        to = lax.rem(me + d, n)
        return pltpu.make_async_remote_copy(
            src_ref=os_ref.at[:, :, block(to)],
            dst_ref=os_all.at[pl.ds(source * seqs, seqs)],
            send_sem=os_send.at[d],
            recv_sem=os_recv.at[source],
            device_id={"dp": to},
            device_id_type=MESH,
        )

    @pl.loop(1, n)
    def _(d):
        slices(d, me).start()

    for j in range(n):
        ti_full[:, j * in_width : (j + 1) * in_width] = ti_ref[j]

    @pl.loop(0, winning)
    def _(i):
        rows[i] = mk_ref[winners_ref[i]]

    token = lax.broadcasted_iota(jnp.int32, (TILE, NQ * TQ), 1)

    @pl.loop(0, tiles)
    def _(t):
        slot = lax.rem(t, 2)
        fetch(t, slot).wait()
        at = pl.ds(pl.multiple_of(t * TILE, TILE), TILE)
        flipped = to_ref[:, at].astype(jnp.float32).T
        for q in range(NQ):
            mine = (token >= q * TQ) & (token < (q + 1) * TQ)
            turned[q] = jnp.where(mine, flipped, 0.0).astype(turned.dtype)

        def piece(c, carry):
            cols = pl.ds(pl.multiple_of(c * span, span), span)
            scale = 1.0 / (eig_buf[slot, :, cols].astype(jnp.float32) + damping)
            for q in range(NQ):
                product = jnp.dot(
                    turned[q], ti_full[:, cols], preferred_element_type=jnp.float32
                )
                precond = (product * scale).astype(jnp.bfloat16)
                right = rows[q * WIN : (q + 1) * WIN, :, cols].reshape(WIN * R, span)
                part = lax.dot_general(
                    right, precond, (((1,), (1,)), ((), ())), preferred_element_type=jnp.float32
                )
                mapped[t, q] = jnp.where(c == 0, part, mapped[t, q] + part)
            return carry

        lax.fori_loop(0, features // span, piece, 0)

        @pl.when(t + 2 < tiles)
        def _():
            fetch(t + 2, slot).start()

    own_slice.wait()

    @pl.loop(1, n)
    def _(d):
        slices(d, me).wait_send()
        slices(d, lax.rem(me + d, n)).wait_recv()

    for i in range(winning):
        q, w = divmod(i, WIN)
        win = winners_ref[i]
        summed = jnp.zeros((R, TILE), jnp.float32)
        for t in range(tiles):
            left = os_all[win, :, t * TILE : (t + 1) * TILE].astype(jnp.float32)
            summed += mapped[t, q, w * R : (w + 1) * R, :] * left
        folded = summed[:, :128]
        for k in range(1, TILE // 128):
            folded += summed[:, k * 128 : (k + 1) * 128]
        lanes[i] = folded
    partial[...] = jnp.sum(lanes[...], axis=2)

    def stage(axis, size, at, source, slots, send_sem, recv_sem):
        own = pltpu.make_async_copy(source, slots.at[at], local_sem.at[1])
        own.start()

        def push(d, slot):
            return pltpu.make_async_remote_copy(
                src_ref=source,
                dst_ref=slots.at[slot],
                send_sem=send_sem.at[d],
                recv_sem=recv_sem.at[slot],
                device_id={axis: lax.rem(at + d, size)},
                device_id_type=MESH,
            )

        @pl.loop(1, size)
        def _(d):
            push(d, at).start()

        own.wait()

        @pl.loop(1, size)
        def _(d):
            push(d, lax.rem(at + d, size)).wait()

        return lax.fori_loop(
            0, size, lambda i, total: total + slots[i], jnp.zeros(slots.shape[1:], slots.dtype)
        )

    sub_total[...] = stage("dp", n, me, partial, dp_slots, dp_send, dp_recv)
    out_ref[...] = stage("layer", layers, my_layer, sub_total, layer_slots, layer_send, layer_recv)


def score(n, layers, winners, turned_out, turned_in, masked, eigenvalues, out_store):
    tokens, width = turned_out.shape
    features = eigenvalues.shape[1]
    count = masked.shape[0]
    winning = winners.shape[0]
    small = (winning, R)
    vmem = pl.BlockSpec(memory_space=pltpu.VMEM)
    anywhere = pl.BlockSpec(memory_space=pl.ANY)
    dma = pltpu.SemaphoreType.DMA
    return pl.pallas_call(
        functools.partial(score_kernel, n, layers),
        out_shape=jax.ShapeDtypeStruct(small, jnp.float32),
        in_specs=[
            pl.BlockSpec(memory_space=pltpu.SMEM), vmem, vmem, vmem, anywhere, anywhere
        ],
        out_specs=vmem,
        scratch_shapes=[
            pltpu.VMEM((count, R, width), jnp.bfloat16),
            pltpu.VMEM((tokens, features), jnp.bfloat16),
            pltpu.VMEM((winning, R, features), jnp.bfloat16),
            pltpu.VMEM((2, TILE, features), jnp.bfloat16),
            pltpu.VMEM((NQ, TILE, tokens), jnp.bfloat16),
            pltpu.VMEM((width // TILE, NQ, WIN * R, TILE), jnp.float32),
            pltpu.VMEM((winning, R, 128), jnp.float32),
            pltpu.VMEM(small, jnp.float32),
            pltpu.VMEM((n, *small), jnp.float32),
            pltpu.VMEM(small, jnp.float32),
            pltpu.VMEM((layers, *small), jnp.float32),
            dma((2,)), dma((2,)), dma((n,)), dma((n,)), dma((n,)), dma((n,)),
            dma((layers,)), dma((layers,)),
        ],
        compiler_params=pltpu.CompilerParams(
            collective_id=1, has_side_effects=True, vmem_limit_bytes=60 << 20
        ),
    )(winners, turned_out, turned_in, masked, eigenvalues, out_store)


def on_device(
    n, layers,
    out_grads, in_acts, out_basis, in_basis, eigenvalues, out_store, in_store, counts, winners
):
    _, seqs, tokens, features = in_store.shape
    alive = (jnp.arange(R, dtype=jnp.int32)[None, :] * SPAN < counts[:, None]).astype(jnp.bfloat16)
    masked = in_store[0] * alive[:, :, None]
    turned_out, turned_in, in_whole = rotate(
        n,
        out_grads[0],
        in_acts[0],
        masked.reshape(seqs * tokens, features),
        out_basis[0],
        in_basis[0],
    )
    totals = score(
        n,
        layers,
        winners.reshape(NQ * WIN),
        turned_out,
        turned_in,
        in_whole.reshape(n * seqs, tokens, features),
        eigenvalues[0],
        out_store[0],
    )
    return totals.reshape(NQ, WIN, R)


def solution(mesh):
    placed = (
        P("layer", None, "dp"),
        P("layer", None, "dp"),
        P("layer", None, "dp"),
        P("layer", None, "dp"),
        P("layer", "dp", None),
        P("layer", "dp", None, None),
        P("layer", "dp", None, None),
        P("dp"),
        P(),
    )
    body = functools.partial(on_device, mesh.shape["dp"], mesh.shape["layer"])
    return jax.shard_map(body, mesh=mesh, in_specs=placed, out_specs=P(), check_vma=False)
```
